32 devices in a mesh: img: 8 (over z, y), band: 4 (over x, core).
Axes of the slice: x: 2, y: 2, z: 4, core: 2. Of those that a mesh axis runs over, the one named last changes fastest.
Arguments:
- patches: bfloat16 [32, 576, 768], P('img', 'band'), may hold values from -6 to 6
- patch_mask: int32 [32, 576], P('img', 'band'), may hold values from 0 to 1, as said below
- band_first: int32 [32, 4], P('img'), may hold values from 0 to 18, as said below
- attn_gain: bfloat16 [768], replicated, may hold values from 0.5 to 1.5
- attn_shift: bfloat16 [768], replicated, may hold values from -3 to 3
- inproj_weight: bfloat16 [768, 2304], replicated, may hold values from -0.21875 to 0.21875
- inproj_bias: bfloat16 [2304], replicated, may hold values from -2 to 2
- rotary_freqs: bfloat16 [2, 12, 32], replicated, may hold values from -3 to 3
- outproj_weight: bfloat16 [768, 768], replicated, may hold values from -0.875 to 0.875
- outproj_bias: bfloat16 [768], replicated, may hold values from -2 to 2
- mlp_gain: bfloat16 [768], replicated, may hold values from 0.5 to 1.5
- mlp_shift: bfloat16 [768], replicated, may hold values from -3 to 3
- expand_weight: bfloat16 [768, 3072], replicated, may hold values from -0.21875 to 0.21875
- expand_bias: bfloat16 [3072], replicated, may hold values from -2 to 2
- reduce_weight: bfloat16 [3072, 768], replicated, may hold values from -0.109375 to 0.109375
- reduce_bias: bfloat16 [768], replicated, may hold values from -2 to 2
- cotangent: bfloat16 [32, 576, 768], P('img', 'band'), may hold values from -6 to 6
Outputs:
- block_out: bfloat16 [32, 576, 768], P('img', 'band')
- d_patches: bfloat16 [32, 576, 768], P('img', 'band')
- grad_attn_gain: float32 [768], P('img')
- grad_attn_shift: float32 [768], P('img')
- grad_inproj_weight: float32 [768, 2304], P('img')
- grad_inproj_bias: float32 [2304], P('img')
- grad_rotary_freqs: float32 [2, 12, 32], replicated
- grad_outproj_weight: float32 [768, 768], P('img')
- grad_outproj_bias: float32 [768], P('img')
- grad_mlp_gain: float32 [768], P('img')
- grad_mlp_shift: float32 [768], P('img')
- grad_expand_weight: float32 [768, 3072], P('img')
- grad_expand_bias: float32 [3072], P('img')
- grad_reduce_weight: float32 [3072, 768], P('img')
- grad_reduce_bias: float32 [768], P('img')
The draws below stay inside these ranges and needn't reach their ends.
Inputs may be any that keep to these rules, and one draw needn't show every extreme that they name: `patch_mask`: each image has a square grid of side 24 * 7 // 12, 20 or 24, and image 0 has side 24; the grid's rows are split over the 4 bands as evenly as possible, earlier bands taking one row more; a slot of local row i and column j of band b is 1 exactly when i is under the band's row count and j under the side. `band_first`: the first patch row of each band of each image, consistent with patch_mask's row counts.
All inputs are finite; a program needn't handle non-finite values.
Results may differ from the reference program's by a relative error of at most 0.012.
The reference program's roundings to bfloat16 on the way count: a program that leaves them out, or rounds other values in their place, can miss the bound.
Values may be sent and summed in bfloat16 or wider, within the bound.
No kernel may reach another device: no remote copies, remote signals or barrier semaphores. Data moves between devices by JAX's collectives and lax.ppermute only.
A program may use at most 192 MiB of HBM per device.

```python
import jax
import jax.numpy as jnp
from jax import lax

D = 768
H = 12
HD = 64
FF = 3072
GRID = 24
IMG_DEV = 4
SLOT_DEV = 144
SLOTS = 576
IMAGES = 32
N_IMG = 8
N_BAND = 4


def image_layout(key):
    side_pick = jax.random.randint(jax.random.fold_in(key, 11), (IMAGES,), 0, 3)
    side_pick = side_pick.at[0].set(2)
    side_table = jnp.array([GRID * 7 // 12, GRID * 5 // 6, GRID], jnp.int32)
    sides = side_table[side_pick]
    band_ids = jnp.arange(N_BAND, dtype=jnp.int32)
    counts = sides[:, None] // N_BAND + (band_ids[None, :] < sides[:, None] % N_BAND).astype(jnp.int32)
    starts = jnp.cumsum(counts, 1) - counts
    return (sides, counts, starts)


def draw_band_first(key, part):
    sides, counts, starts = image_layout(key)
    return starts.astype(jnp.int32)


def draw_patch_mask(key, part):
    sides, counts, starts = image_layout(key)
    slot_index = jnp.arange(SLOTS, dtype=jnp.int32)
    band_of = slot_index // SLOT_DEV
    row_in = slot_index % SLOT_DEV // GRID
    col_in = slot_index % GRID
    live = (row_in[None, :] < counts[:, band_of]) & (col_in[None, :] < sides[:, None])
    return live.astype(jnp.int32)


def shard_levels(stream_key, extent, split, smallest, largest):
    loudness = 1.0
    for axis_at, blocks in split:
        steps = jax.random.uniform(jax.random.fold_in(jax.random.fold_in(stream_key, 6), axis_at), (blocks,), jnp.float32, smallest / len(split), largest / len(split))
        loudness = loudness * jnp.repeat(jnp.exp(steps), extent[axis_at] // blocks).reshape((-1,) + (1,) * (len(extent) - 1 - axis_at))
    return loudness


def centred(key, extent, deviation, bound, cuts=(), held_as=jnp.bfloat16):
    values = jax.random.normal(key, extent, jnp.float32) * deviation
    if len(cuts) > 0:
        values = shard_levels(key, extent, cuts, -0.22, 0.18) * values
    return jnp.clip(values, min=-bound, max=bound).astype(held_as)


def setup_inputs(seed: int = 0) -> dict:
    splits = jax.random.split(jax.random.key(seed), 18)
    patches = centred(splits[0], (IMAGES, SLOTS, D), 1.0, 6.0, ((0, 8), (1, 4)))
    patch_mask = draw_patch_mask(jax.random.fold_in(splits[17], 71), 0)
    band_first = draw_band_first(jax.random.fold_in(splits[17], 71), 0)
    attn_gain = jnp.clip(1.0 + 0.1 * jax.random.normal(splits[3], (D,), jnp.float32), 0.5, 1.5).astype(jnp.bfloat16)
    attn_shift = centred(splits[4], (D,), 0.5, 3.0)
    inproj_weight = centred(splits[5], (D, 3 * D), D ** -0.5, 0.21875)
    inproj_bias = centred(splits[6], (3 * D,), 0.3, 2.0)
    rotary_freqs = centred(splits[7], (2, H, HD // 2), 0.5, 3.0)
    outproj_weight = centred(splits[8], (D, D), (D // 16) ** -0.5, 0.875)
    outproj_bias = centred(splits[9], (D,), 0.3, 2.0)
    mlp_gain = jnp.clip(1.0 + 0.1 * jax.random.normal(splits[10], (D,), jnp.float32), 0.5, 1.5).astype(jnp.bfloat16)
    mlp_shift = centred(splits[11], (D,), 0.5, 3.0)
    expand_weight = centred(splits[12], (D, FF), D ** -0.5, 0.21875)
    expand_bias = centred(splits[13], (FF,), 0.3, 2.0)
    reduce_weight = centred(splits[14], (FF, D), FF ** -0.5, 0.109375)
    reduce_bias = centred(splits[15], (D,), 0.3, 2.0)
    cotangent = centred(splits[16], (IMAGES, SLOTS, D), 1.0, 6.0, ((0, 8), (1, 4)))
    return dict(patches=patches, patch_mask=patch_mask, band_first=band_first, attn_gain=attn_gain, attn_shift=attn_shift, inproj_weight=inproj_weight, inproj_bias=inproj_bias, rotary_freqs=rotary_freqs, outproj_weight=outproj_weight, outproj_bias=outproj_bias, mlp_gain=mlp_gain, mlp_shift=mlp_shift, expand_weight=expand_weight, expand_bias=expand_bias, reduce_weight=reduce_weight, reduce_bias=reduce_bias, cotangent=cotangent)


EPS = 1e-06
NEG = -1e+30

@jax.custom_vjp
def low(v):
    return lax.optimization_barrier(v.astype(jnp.bfloat16)).astype(jnp.float32)

@jax.custom_vjp
def low_back(v):
    return v

def low_keep(v):
    return (low(v), None)

def low_pass(kept, grad):
    return (grad,)

def back_keep(v):
    return (v, None)

def back_low(kept, grad):
    return (low(grad),)
low.defvjp(low_keep, low_pass)
low_back.defvjp(back_keep, back_low)

def layer_norm(values, gain, shift):
    center = values - lax.optimization_barrier(jnp.mean(values, -1, keepdims=True))
    spread = lax.optimization_barrier(jnp.mean(center * center, -1, keepdims=True))
    return center * lax.rsqrt(spread + EPS) * gain + shift

def rotate(tensor, cosine, sine):
    half_size = tensor.shape[-1] // 2
    first_half = tensor[..., :half_size]
    second_half = tensor[..., half_size:]
    return jnp.concatenate([first_half * cosine - second_half * sine, first_half * sine + second_half * cosine], -1)

def matmul(left, right):
    return jnp.einsum('isd,de->ise', left, right, precision=lax.Precision.HIGHEST)

def forward(weights, patches, real_slot, band_first):
    attn_gain, attn_shift, inproj_weight, inproj_bias, rotary_freqs, outproj_weight, outproj_bias, mlp_gain, mlp_shift, expand_weight, expand_bias, reduce_weight, reduce_bias = weights
    image_count, slot_count, model_width = patches.shape
    head_count = rotary_freqs.shape[1]
    head_size = model_width // head_count
    highest = lax.Precision.HIGHEST
    slot_index = jnp.arange(slot_count)
    starts = band_first[:, slot_index // SLOT_DEV]
    patch_rows = (starts + (slot_index % SLOT_DEV // GRID)[None, :]).astype(jnp.float32)
    patch_cols = jnp.broadcast_to((slot_index % GRID).astype(jnp.float32)[None, :], patch_rows.shape)
    attn_in = low(layer_norm(patches, attn_gain, attn_shift))
    projected = low_back(matmul(attn_in, inproj_weight) + inproj_bias)
    shaped = projected.reshape(image_count, slot_count, 3, head_count, head_size)
    angles = patch_rows[..., None, None] * rotary_freqs[0] + patch_cols[..., None, None] * rotary_freqs[1]
    cosine = jnp.cos(angles)
    sine = jnp.sin(angles)
    query_rot = low(rotate(shaped[:, :, 0], cosine, sine))
    key_rot = low(rotate(shaped[:, :, 1], cosine, sine))
    value_low = low(shaped[:, :, 2])
    score_scale = head_size ** (-0.5)
    scores = low_back(jnp.einsum('ishd,ithd->ihst', query_rot, key_rot, precision=highest) * score_scale)
    visible = real_slot[:, None, None, :] > 0
    masked = jnp.where(visible, scores, NEG)
    row_max = lax.optimization_barrier(jnp.max(masked, -1, keepdims=True))
    expo = jnp.exp(masked - row_max)
    soft_probs = expo / lax.optimization_barrier(jnp.sum(expo, -1, keepdims=True))
    attn_mix = low(low_back(jnp.einsum('ihst,ithd->ishd', low(soft_probs), value_low, precision=highest)))
    attn_mix = attn_mix.reshape(image_count, slot_count, model_width)
    resid_mid = patches + low_back(matmul(attn_mix, outproj_weight) + outproj_bias)
    mlp_in = low(layer_norm(resid_mid, mlp_gain, mlp_shift))
    pre_act = low_back(matmul(mlp_in, expand_weight) + expand_bias)
    hidden = low(jax.nn.gelu(pre_act, approximate=False))
    branch = low_back(matmul(hidden, reduce_weight) + reduce_bias)
    return real_slot[..., None] * (resid_mid + branch)

def reference(patches, patch_mask, band_first, attn_gain, attn_shift, inproj_weight, inproj_bias, rotary_freqs, outproj_weight, outproj_bias, mlp_gain, mlp_shift, expand_weight, expand_bias, reduce_weight, reduce_bias, cotangent):
    weights = tuple((item.astype(jnp.float32) for item in (attn_gain, attn_shift, inproj_weight, inproj_bias, rotary_freqs, outproj_weight, outproj_bias, mlp_gain, mlp_shift, expand_weight, expand_bias, reduce_weight, reduce_bias)))
    blocks = (patches.astype(jnp.float32).reshape(N_IMG, IMG_DEV, SLOTS, D), patch_mask.astype(jnp.float32).reshape(N_IMG, IMG_DEV, SLOTS), band_first.astype(jnp.int32).reshape(N_IMG, IMG_DEV, N_BAND), cotangent.astype(jnp.float32).reshape(N_IMG, IMG_DEV, SLOTS, D))

    def step(totals, block):
        block_x, block_mask, block_first, block_cot = block
        result, pull = jax.vjp(lambda weight_set, inputs: forward(weight_set, inputs, block_mask, block_first), weights, block_x)
        grad_weights, grad_x = pull(block_cot)
        totals = tuple((acc + extra for acc, extra in zip(totals, grad_weights)))
        return (totals, (result.astype(jnp.bfloat16), grad_x.astype(jnp.bfloat16)))
    zeros = tuple((jnp.zeros(item.shape, jnp.float32) for item in weights))
    totals, (outputs, grads_in) = lax.scan(step, zeros, blocks)
    return (outputs.reshape(IMAGES, SLOTS, D), grads_in.reshape(IMAGES, SLOTS, D), totals[0], totals[1], totals[2], totals[3], totals[4], totals[5], totals[6], totals[7], totals[8], totals[9], totals[10], totals[11], totals[12])
```

```python
import jax
import jax.numpy as jnp
from jax import lax
from jax.sharding import PartitionSpec as P

GRID = 24
EPS = 1e-06
NEG = -1e30


def norm_parts(values):
    center = values - jnp.mean(values, -1, keepdims=True)
    rstd = lax.rsqrt(jnp.mean(center * center, -1, keepdims=True) + EPS)
    return center * rstd, rstd


def norm_back(grad, gain, xhat, rstd):
    scaled = grad * gain
    inner = jnp.mean(scaled * xhat, -1, keepdims=True)
    return rstd * (scaled - jnp.mean(scaled, -1, keepdims=True) - xhat * inner)


def turn(tensor, cosine, sine):
    half = tensor.shape[-1] // 2
    first, second = tensor[..., :half], tensor[..., half:]
    return jnp.concatenate(
        [first * cosine - second * sine, first * sine + second * cosine], -1
    )


def matrix_sum(grad):
    low = grad.astype(jnp.bfloat16)
    low = lax.psum_scatter(low, "band", scatter_dimension=1, tiled=True)
    low = lax.psum_scatter(low, "img", scatter_dimension=0, tiled=True)
    low = lax.all_gather(low, "band", axis=1, tiled=True)
    return low.astype(jnp.float32)


def local(
    patches,
    patch_mask,
    band_first,
    attn_gain,
    attn_shift,
    inproj_weight,
    inproj_bias,
    rotary_freqs,
    outproj_weight,
    outproj_bias,
    mlp_gain,
    mlp_shift,
    expand_weight,
    expand_bias,
    reduce_weight,
    reduce_bias,
    cotangent,
):
    single = jnp.float32
    low = jnp.bfloat16
    images, slots, width = patches.shape
    heads = rotary_freqs.shape[1]
    size = width // heads
    scale = size ** (-0.5)
    bands = lax.axis_size("band")
    here = lax.axis_index("band")

    def gather_image(values):
        return lax.all_to_all(values, "band", 0, 1, tiled=True)

    def spread_image(values):
        return lax.all_to_all(values, "band", 1, 0, tiled=True)

    patches = gather_image(patches)
    cotangent = gather_image(cotangent)
    mask = gather_image(patch_mask).astype(single)
    count = images // bands
    total = slots * bands
    starts = lax.dynamic_slice_in_dim(band_first, here * count, count, 0)
    row_in = jnp.arange(slots) // GRID
    rows = (starts[:, :, None] + row_in[None, None, :]).reshape(count, total).astype(single)
    cols = jnp.broadcast_to(
        (jnp.arange(total) % GRID).astype(single)[None, :], rows.shape
    )
    freqs = rotary_freqs.astype(single)
    angles = rows[..., None, None] * freqs[0] + cols[..., None, None] * freqs[1]
    cosine, sine = jnp.cos(angles), jnp.sin(angles)

    wide = patches.astype(single)
    xhat_one, rstd_one = norm_parts(wide)
    gain_one = attn_gain.astype(single)
    attn_in = (xhat_one * gain_one + attn_shift.astype(single)).astype(low)
    projected = jnp.dot(attn_in, inproj_weight, preferred_element_type=single)
    projected = projected + inproj_bias.astype(single)
    split = projected.reshape(count, total, 3, heads, size)
    query_rot = turn(split[:, :, 0], cosine, sine).astype(low)
    key_rot = turn(split[:, :, 1], cosine, sine).astype(low)
    value_low = split[:, :, 2].astype(low)
    scores = jnp.einsum("iqhd,ikhd->ihqk", query_rot, key_rot, preferred_element_type=single)
    masked = jnp.where(mask[:, None, None, :] > 0, scores * scale, NEG)
    expo = jnp.exp(masked - jnp.max(masked, -1, keepdims=True))
    probs = expo / jnp.sum(expo, -1, keepdims=True)
    probs_low = probs.astype(low)
    mix = jnp.einsum("ihqk,ikhd->iqhd", probs_low, value_low, preferred_element_type=single)
    mix = mix.reshape(count, total, width).astype(low)
    attn_out = jnp.dot(mix, outproj_weight, preferred_element_type=single)
    resid_mid = wide + attn_out + outproj_bias.astype(single)
    xhat_two, rstd_two = norm_parts(resid_mid)
    gain_two = mlp_gain.astype(single)
    mlp_in = (xhat_two * gain_two + mlp_shift.astype(single)).astype(low)
    pre_act = jnp.dot(mlp_in, expand_weight, preferred_element_type=single)
    pre_act = pre_act + expand_bias.astype(single)
    half_erf = 0.5 + 0.5 * lax.erf(pre_act * (0.5**0.5))
    hidden = (pre_act * half_erf).astype(low)
    slope = half_erf + pre_act * jnp.exp(-0.5 * pre_act * pre_act) * 0.3989422804014327
    branch = jnp.dot(hidden, reduce_weight, preferred_element_type=single)
    block_out = mask[..., None] * (resid_mid + branch + reduce_bias.astype(single))
    block_out = spread_image(block_out.astype(low))

    grad_top = cotangent.astype(single) * mask[..., None]
    grad_low = grad_top.astype(low)
    grad_reduce_weight = jnp.einsum("iqf,iqd->fd", hidden, grad_low, preferred_element_type=single)
    grad_reduce_bias = jnp.sum(grad_top, (0, 1))
    d_hidden = jnp.einsum("iqd,fd->iqf", grad_low, reduce_weight, preferred_element_type=single)
    d_pre = (d_hidden * slope).astype(low)
    grad_expand_weight = jnp.einsum("iqd,iqf->df", mlp_in, d_pre, preferred_element_type=single)
    grad_expand_bias = jnp.sum(d_pre.astype(single), (0, 1))
    d_mlp_in = jnp.einsum("iqf,df->iqd", d_pre, expand_weight, preferred_element_type=single)
    grad_mlp_gain = jnp.sum(d_mlp_in * xhat_two, (0, 1))
    grad_mlp_shift = jnp.sum(d_mlp_in, (0, 1))
    d_mid = grad_top + norm_back(d_mlp_in, gain_two, xhat_two, rstd_two)
    d_attn = d_mid.astype(low)
    grad_outproj_weight = jnp.einsum("iqe,iqd->ed", mix, d_attn, preferred_element_type=single)
    grad_outproj_bias = jnp.sum(d_attn.astype(single), (0, 1))
    d_mix = jnp.einsum("iqd,ed->iqe", d_attn, outproj_weight, preferred_element_type=single)
    d_mix = d_mix.astype(low).reshape(count, total, heads, size)
    d_values = jnp.einsum("ihqk,iqhd->ikhd", probs_low, d_mix, preferred_element_type=single)
    d_probs = jnp.einsum("iqhd,ikhd->ihqk", d_mix, value_low, preferred_element_type=single)
    inner = jnp.sum(probs * d_probs, -1, keepdims=True)
    d_scores = (probs * (d_probs - inner)).astype(low)
    d_qrot = scale * jnp.einsum("ihqk,ikhd->iqhd", d_scores, key_rot, preferred_element_type=single)
    d_krot = scale * jnp.einsum("ihqk,iqhd->ikhd", d_scores, query_rot, preferred_element_type=single)
    half = size // 2
    slope_q = d_qrot[..., half:] * query_rot[..., :half] - d_qrot[..., :half] * query_rot[..., half:]
    slope_k = d_krot[..., half:] * key_rot[..., :half] - d_krot[..., :half] * key_rot[..., half:]
    d_angle = slope_q + slope_k
    grad_freqs = jnp.stack(
        [
            jnp.sum(rows[..., None, None] * d_angle, (0, 1)),
            jnp.sum(cols[..., None, None] * d_angle, (0, 1)),
        ]
    )
    d_queries = turn(d_qrot, cosine, -sine)
    d_keys = turn(d_krot, cosine, -sine)
    flat = (count, total, width)
    d_proj = jnp.concatenate(
        [d_queries.reshape(flat), d_keys.reshape(flat), d_values.reshape(flat)], -1
    ).astype(low)
    grad_inproj_weight = jnp.einsum("iqd,iqe->de", attn_in, d_proj, preferred_element_type=single)
    grad_inproj_bias = jnp.sum(d_proj.astype(single), (0, 1))
    d_attn_in = jnp.einsum("iqe,de->iqd", d_proj, inproj_weight, preferred_element_type=single)
    grad_attn_gain = jnp.sum(d_attn_in * xhat_one, (0, 1))
    grad_attn_shift = jnp.sum(d_attn_in, (0, 1))
    d_patches = d_mid + norm_back(d_attn_in, gain_one, xhat_one, rstd_one)
    d_patches = spread_image(d_patches.astype(low))

    small = (
        grad_attn_gain,
        grad_attn_shift,
        grad_inproj_bias,
        grad_outproj_bias,
        grad_mlp_gain,
        grad_mlp_shift,
        grad_expand_bias,
        grad_reduce_bias,
        grad_freqs.reshape(-1),
    )
    packed = lax.psum(jnp.concatenate(small), ("img", "band"))
    shares = lax.axis_size("img")
    mine = lax.axis_index("img")
    sums = []
    at = 0
    for piece in small:
        long = piece.shape[0]
        sums.append(packed[at : at + long])
        at += long
    freq_total = sums.pop().reshape(grad_freqs.shape)
    sums = [
        lax.dynamic_slice_in_dim(s, mine * (s.shape[0] // shares), s.shape[0] // shares)
        for s in sums
    ]
    return (
        block_out,
        d_patches,
        sums[0],
        sums[1],
        matrix_sum(grad_inproj_weight),
        sums[2],
        freq_total,
        matrix_sum(grad_outproj_weight),
        sums[3],
        sums[4],
        sums[5],
        matrix_sum(grad_expand_weight),
        sums[6],
        matrix_sum(grad_reduce_weight),
        sums[7],
    )


def solution(mesh):
    act = P("img", "band", None)
    row = P("img")
    mat = P("img", None)
    return jax.shard_map(
        local,
        mesh=mesh,
        in_specs=(act, P("img", "band"), P("img", None)) + (P(),) * 13 + (act,),
        out_specs=(act, act, row, row, mat, row, P(), mat, row, row, row, mat, row, mat, row),
        check_vma=False,
    )
```

```python
import jax
import jax.numpy as jnp
from jax import lax
from jax.sharding import PartitionSpec as P

GRID = 24
EPS = 1e-06
NEG = -1e30


def norm_parts(values):
    center = values - jnp.mean(values, -1, keepdims=True)
    rstd = lax.rsqrt(jnp.mean(center * center, -1, keepdims=True) + EPS)
    return center * rstd, rstd


def norm_back(grad, gain, xhat, rstd):
    scaled = grad * gain
    inner = jnp.mean(scaled * xhat, -1, keepdims=True)
    return rstd * (scaled - jnp.mean(scaled, -1, keepdims=True) - xhat * inner)


def turn(tensor, cosine, sine):
    half = tensor.shape[-1] // 2
    first, second = tensor[..., :half], tensor[..., half:]
    return jnp.concatenate(
        [first * cosine - second * sine, first * sine + second * cosine], -1
    )


def swap(values, axis, bit):
    total = lax.axis_size(axis)
    return lax.ppermute(values, axis, [(i, i ^ bit) for i in range(total)])


def halve(values, axis, bit, at):
    mine = (lax.axis_index(axis) // bit) % 2
    away = lax.dynamic_index_in_dim(values, 1 - mine, at, keepdims=False)
    kept = lax.dynamic_index_in_dim(values, mine, at, keepdims=False)
    single = jnp.float32
    got = swap(away, axis, bit)
    return (kept.astype(single) + got.astype(single)).astype(values.dtype)


def join(values, axis, bit, at):
    mine = (lax.axis_index(axis) // bit) % 2
    got = swap(values, axis, bit)
    first = jnp.where(mine == 0, values, got)
    second = jnp.where(mine == 0, got, values)
    return jnp.concatenate([first, second], at)


def matrix_sum(left, right):
    single, low = jnp.float32, jnp.bfloat16
    shares = lax.axis_size("img")
    core = lax.axis_index("band") % 2
    half = right.shape[1] // 2

    def product(which):
        part = lax.dynamic_slice_in_dim(right, which * half, half, 1)
        return jnp.einsum("qa,qb->ab", left, part, preferred_element_type=single).astype(low)

    got = swap(product(1 - core), "band", 1)
    total = (product(core).astype(single) + got.astype(single)).astype(low)
    depth = left.shape[1] // shares
    total = halve(total.reshape(shares, 2, depth // 2, half), "band", 2, 1)
    bit = 1
    while bit < shares:
        total = total.reshape(shares // (2 * bit), 2, depth // 2, half)
        total = halve(total, "img", bit, 1)
        bit *= 2
    total = total.reshape(depth // 2, half)
    total = join(total, "band", 2, 0)
    total = join(total, "band", 1, 1)
    return total.astype(single)


def vector_sum(values):
    for axis in ("band", "img"):
        bit = 1
        while bit < lax.axis_size(axis):
            values = values + swap(values, axis, bit)
            bit *= 2
    return values


def local(
    patches,
    patch_mask,
    band_first,
    attn_gain,
    attn_shift,
    inproj_weight,
    inproj_bias,
    rotary_freqs,
    outproj_weight,
    outproj_bias,
    mlp_gain,
    mlp_shift,
    expand_weight,
    expand_bias,
    reduce_weight,
    reduce_bias,
    cotangent,
):
    single = jnp.float32
    low = jnp.bfloat16
    images, slots, width = patches.shape
    heads = rotary_freqs.shape[1]
    size = width // heads
    scale = size ** (-0.5)
    bands = lax.axis_size("band")
    here = lax.axis_index("band")

    def gather_image(values):
        return lax.all_to_all(values, "band", 0, 1, tiled=True)

    def spread_image(values):
        return lax.all_to_all(values, "band", 1, 0, tiled=True)

    def flatten(values):
        return values.reshape(-1, values.shape[-1])

    patches = gather_image(patches)
    cotangent = gather_image(cotangent)
    count = images // bands
    total = slots * bands
    starts = lax.dynamic_slice_in_dim(band_first, here * count, count, 0)
    row_in = jnp.arange(slots) // GRID
    side = 4 * starts[:, -1:] // 3
    counts = jnp.concatenate([starts[:, 1:], side], 1) - starts
    live = (row_in[None, None, :] < counts[:, :, None]) & (
        jnp.arange(slots)[None, None, :] % GRID < side[:, :, None]
    )
    mask = live.reshape(count, total).astype(single)
    rows = (starts[:, :, None] + row_in[None, None, :]).reshape(count, total).astype(single)
    cols = jnp.broadcast_to(
        (jnp.arange(total) % GRID).astype(single)[None, :], rows.shape
    )
    freqs = rotary_freqs.astype(single)
    angles = rows[..., None, None] * freqs[0] + cols[..., None, None] * freqs[1]
    cosine, sine = jnp.cos(angles), jnp.sin(angles)

    wide = patches.astype(single)
    xhat_one, rstd_one = norm_parts(wide)
    gain_one = attn_gain.astype(single)
    attn_in = (xhat_one * gain_one + attn_shift.astype(single)).astype(low)
    projected = jnp.dot(attn_in, inproj_weight, preferred_element_type=single)
    projected = projected + inproj_bias.astype(single)
    split = projected.reshape(count, total, 3, heads, size)
    query_rot = turn(split[:, :, 0], cosine, sine).astype(low)
    key_rot = turn(split[:, :, 1], cosine, sine).astype(low)
    value_low = split[:, :, 2].astype(low)
    scores = jnp.einsum("iqhd,ikhd->ihqk", query_rot, key_rot, preferred_element_type=single)
    masked = jnp.where(mask[:, None, None, :] > 0, scores * scale, NEG)
    expo = jnp.exp(masked - jnp.max(masked, -1, keepdims=True))
    probs = expo / jnp.sum(expo, -1, keepdims=True)
    probs_low = probs.astype(low)
    mix = jnp.einsum("ihqk,ikhd->iqhd", probs_low, value_low, preferred_element_type=single)
    mix = mix.reshape(count, total, width).astype(low)
    attn_out = jnp.dot(mix, outproj_weight, preferred_element_type=single)
    resid_mid = wide + attn_out + outproj_bias.astype(single)
    xhat_two, rstd_two = norm_parts(resid_mid)
    gain_two = mlp_gain.astype(single)
    mlp_in = (xhat_two * gain_two + mlp_shift.astype(single)).astype(low)
    pre_act = jnp.dot(mlp_in, expand_weight, preferred_element_type=single)
    pre_act = pre_act + expand_bias.astype(single)
    half_erf = 0.5 + 0.5 * lax.erf(pre_act * (0.5**0.5))
    hidden = (pre_act * half_erf).astype(low)
    slope = half_erf + pre_act * jnp.exp(-0.5 * pre_act * pre_act) * 0.3989422804014327
    branch = jnp.dot(hidden, reduce_weight, preferred_element_type=single)
    block_out = mask[..., None] * (resid_mid + branch + reduce_bias.astype(single))
    block_out = spread_image(block_out.astype(low))

    grad_top = cotangent.astype(single) * mask[..., None]
    grad_low = grad_top.astype(low)
    grad_reduce_weight = matrix_sum(flatten(hidden), flatten(grad_low))
    grad_reduce_bias = jnp.sum(grad_top, (0, 1))
    d_hidden = jnp.einsum("iqd,fd->iqf", grad_low, reduce_weight, preferred_element_type=single)
    d_pre = (d_hidden * slope).astype(low)
    grad_expand_weight = matrix_sum(flatten(mlp_in), flatten(d_pre))
    grad_expand_bias = jnp.sum(d_pre.astype(single), (0, 1))
    d_mlp_in = jnp.einsum("iqf,df->iqd", d_pre, expand_weight, preferred_element_type=single)
    grad_mlp_gain = jnp.sum(d_mlp_in * xhat_two, (0, 1))
    grad_mlp_shift = jnp.sum(d_mlp_in, (0, 1))
    d_mid = grad_top + norm_back(d_mlp_in, gain_two, xhat_two, rstd_two)
    d_attn = d_mid.astype(low)
    grad_outproj_weight = matrix_sum(flatten(mix), flatten(d_attn))
    grad_outproj_bias = jnp.sum(d_attn.astype(single), (0, 1))
    d_mix = jnp.einsum("iqd,ed->iqe", d_attn, outproj_weight, preferred_element_type=single)
    d_mix = d_mix.astype(low).reshape(count, total, heads, size)
    d_values = jnp.einsum("ihqk,iqhd->ikhd", probs_low, d_mix, preferred_element_type=single)
    d_probs = jnp.einsum("iqhd,ikhd->ihqk", d_mix, value_low, preferred_element_type=single)
    inner = jnp.sum(probs * d_probs, -1, keepdims=True)
    d_scores = (probs * (d_probs - inner)).astype(low)
    d_qrot = scale * jnp.einsum("ihqk,ikhd->iqhd", d_scores, key_rot, preferred_element_type=single)
    d_krot = scale * jnp.einsum("ihqk,iqhd->ikhd", d_scores, query_rot, preferred_element_type=single)
    half = size // 2
    slope_q = d_qrot[..., half:] * query_rot[..., :half] - d_qrot[..., :half] * query_rot[..., half:]
    slope_k = d_krot[..., half:] * key_rot[..., :half] - d_krot[..., :half] * key_rot[..., half:]
    d_angle = slope_q + slope_k
    grad_freqs = jnp.stack(
        [
            jnp.sum(rows[..., None, None] * d_angle, (0, 1)),
            jnp.sum(cols[..., None, None] * d_angle, (0, 1)),
        ]
    )
    d_queries = turn(d_qrot, cosine, -sine)
    d_keys = turn(d_krot, cosine, -sine)
    flat = (count, total, width)
    d_proj = jnp.concatenate(
        [d_queries.reshape(flat), d_keys.reshape(flat), d_values.reshape(flat)], -1
    ).astype(low)
    grad_inproj_weight = matrix_sum(flatten(attn_in), flatten(d_proj))
    grad_inproj_bias = jnp.sum(d_proj.astype(single), (0, 1))
    d_attn_in = jnp.einsum("iqe,de->iqd", d_proj, inproj_weight, preferred_element_type=single)
    grad_attn_gain = jnp.sum(d_attn_in * xhat_one, (0, 1))
    grad_attn_shift = jnp.sum(d_attn_in, (0, 1))
    d_patches = d_mid + norm_back(d_attn_in, gain_one, xhat_one, rstd_one)
    d_patches = spread_image(d_patches.astype(low))

    small = (
        grad_attn_gain,
        grad_attn_shift,
        grad_inproj_bias,
        grad_outproj_bias,
        grad_mlp_gain,
        grad_mlp_shift,
        grad_expand_bias,
        grad_reduce_bias,
        grad_freqs.reshape(-1),
    )
    packed = vector_sum(jnp.concatenate(small))
    shares = lax.axis_size("img")
    mine = lax.axis_index("img")
    sums = []
    at = 0
    for piece in small:
        long = piece.shape[0]
        sums.append(packed[at : at + long])
        at += long
    freq_total = sums.pop().reshape(grad_freqs.shape)
    sums = [
        lax.dynamic_slice_in_dim(s, mine * (s.shape[0] // shares), s.shape[0] // shares)
        for s in sums
    ]
    return (
        block_out,
        d_patches,
        sums[0],
        sums[1],
        grad_inproj_weight,
        sums[2],
        freq_total,
        grad_outproj_weight,
        sums[3],
        sums[4],
        sums[5],
        grad_expand_weight,
        sums[6],
        grad_reduce_weight,
        sums[7],
    )


def solution(mesh):
    act = P("img", "band", None)
    row = P("img")
    mat = P("img", None)
    return jax.shard_map(
        local,
        mesh=mesh,
        in_specs=(act, P("img", "band"), P("img", None)) + (P(),) * 13 + (act,),
        out_specs=(act, act, row, row, mat, row, P(), mat, row, row, row, mat, row, mat, row),
        check_vma=False,
    )
```

```python
import jax
import jax.numpy as jnp
from jax import lax
from jax.experimental import pallas as pl
from jax.experimental.pallas import tpu as pltpu
from jax.sharding import PartitionSpec as P

GRID = 24
EPS = 1e-06
NEG = -1e30


def norm_parts(values):
    center = values - jnp.mean(values, -1, keepdims=True)
    rstd = lax.rsqrt(jnp.mean(center * center, -1, keepdims=True) + EPS)
    return center * rstd, rstd


def norm_back(grad, gain, xhat, rstd):
    scaled = grad * gain
    inner = jnp.mean(scaled * xhat, -1, keepdims=True)
    return rstd * (scaled - jnp.mean(scaled, -1, keepdims=True) - xhat * inner)


GROUP = 256


def contract(left, right, left_dim, right_dim):
    return lax.dot_general(
        left, right, (((left_dim,), (right_dim,)), ((), ())), preferred_element_type=jnp.float32
    )


def partner(values, low_half):
    wide = values.shape[-1]
    return jnp.where(
        low_half, pltpu.roll(values, wide - 32, 1), pltpu.roll(values, 32, 1)
    )


def angle_tables(tables):
    row_cos, row_sin, col_cos, col_sin = (tables[i] for i in range(4))
    count, wide = row_cos.shape
    rc, rs = row_cos[:, None, :], row_sin[:, None, :]
    cc, cs = col_cos[None, :, :], col_sin[None, :, :]
    cosine = (rc * cc - rs * cs).reshape(count * count, wide)
    sine = (rs * cc + rc * cs).reshape(count * count, wide)
    return cosine, sine


def lane_masks(slots):
    lane = lax.broadcasted_iota(jnp.int32, (slots, GROUP), 1)
    return lane % 64 < 32


def attend_kernel(
    x_ref, wq_ref, wk_ref, wv_ref, b_ref, tab_ref, bias_ref, q_ref, k_ref, v_ref, mix_ref, p_ref
):
    low, single = jnp.bfloat16, jnp.float32
    slots = x_ref.shape[0]
    cosine, sine = angle_tables(tab_ref)
    low_half = lane_masks(slots)
    signed = jnp.where(low_half, -sine, sine)
    x = x_ref[...]

    def projected(w_ref, at):
        return jnp.dot(x, w_ref[...], preferred_element_type=single) + b_ref[at].astype(single)

    q = projected(wq_ref, 0)
    q_ref[...] = ((q * cosine + partner(q, low_half) * signed)).astype(low)
    k = projected(wk_ref, 1)
    k_ref[...] = (k * cosine + partner(k, low_half) * signed).astype(low)
    v_ref[...] = projected(wv_ref, 2).astype(low)
    hide = bias_ref[...]
    lane = lax.broadcasted_iota(jnp.int32, (slots, 128), 1)
    for pair in range(GROUP // 128):
        cols = slice(pair * 128, pair * 128 + 128)
        q = q_ref[:, cols] * jnp.asarray(0.125, low)
        k = k_ref[:, cols]
        v_turned = v_ref[:, cols].T
        parts = []
        for head in range(2):
            own = (lane < 64) if head == 0 else (lane >= 64)
            scores = contract(k, jnp.where(own, q, jnp.zeros_like(q)), 1, 1) + hide
            expo = jnp.exp(scores - jnp.max(scores, 0, keepdims=True))
            probs = (expo * (1.0 / jnp.sum(expo, 0, keepdims=True))).astype(low)
            p_ref[pair * 2 + head] = probs
            rows = slice(head * 64, head * 64 + 64)
            parts.append(jnp.dot(v_turned[rows], probs, preferred_element_type=single))
        mix_ref[:, cols] = jnp.concatenate(parts, 0).T.astype(low)


def attend(attn_in, weight, bias, tables, hide):
    slots, width = attn_in.shape
    steps = width // GROUP
    low = jnp.bfloat16

    def part(at):
        return pl.BlockSpec((width, GROUP), lambda j: (0, at * steps + j))

    cols = pl.BlockSpec((slots, GROUP), lambda j: (0, j))
    act = jax.ShapeDtypeStruct((slots, width), low)
    heads = GROUP // 64
    return pl.pallas_call(
        attend_kernel,
        grid=(steps,),
        in_specs=[
            pl.BlockSpec((slots, width), lambda j: (0, 0)),
            part(0),
            part(1),
            part(2),
            pl.BlockSpec((3, 1, GROUP), lambda j: (0, 0, j)),
            pl.BlockSpec((4, GRID, GROUP), lambda j: (0, 0, j)),
            pl.BlockSpec((slots, 1), lambda j: (0, 0)),
        ],
        out_specs=[cols] * 4 + [pl.BlockSpec((heads, slots, slots), lambda j: (j, 0, 0))],
        out_shape=[act] * 4 + [jax.ShapeDtypeStruct((width // 64, slots, slots), low)],
        cost_estimate=pl.CostEstimate(
            flops=6 * slots * width * width + 4 * slots * slots * width,
            bytes_accessed=3 * width * width * 2 + slots * slots * 24,
            transcendentals=slots * slots * 12,
        ),
        name="attend",
    )(attn_in, weight, weight, weight, bias.reshape(3, 1, width), tables, hide)


def attend_back_kernel(
    g_ref, wo_ref, q_ref, k_ref, v_ref, p_ref, tab_ref, row_ref, dq_ref, dk_ref, dv_ref, sum_ref
):
    low, single = jnp.bfloat16, jnp.float32
    slots = g_ref.shape[0]
    d_mix = contract(g_ref[...], wo_ref[...], 1, 1).astype(low)
    lane = lax.broadcasted_iota(jnp.int32, (slots, 128), 1)
    zero = jnp.zeros((slots, 128), low)
    d_q, d_k = [], []
    for pair in range(GROUP // 128):
        cols = slice(pair * 128, pair * 128 + 128)
        q, k, v = q_ref[:, cols], k_ref[:, cols], v_ref[:, cols]
        grad = d_mix[:, cols]
        k_turned = k.T
        d_v_parts, d_k_parts, d_q_parts = [], [], []
        for head in range(2):
            own = (lane < 64) if head == 0 else (lane >= 64)
            probs = p_ref[pair * 2 + head]
            wide = probs.astype(single)
            d_probs = contract(v, jnp.where(own, grad, zero), 1, 1)
            weighed = wide * d_probs
            inner = jnp.sum(weighed, 0, keepdims=True)
            d_scores = (weighed - wide * inner).astype(low)
            d_v_parts.append(jnp.dot(probs, grad, preferred_element_type=single))
            d_k_parts.append(jnp.dot(d_scores, q, preferred_element_type=single))
            rows = slice(head * 64, head * 64 + 64)
            d_q_parts.append(jnp.dot(k_turned[rows], d_scores, preferred_element_type=single))
        dv_ref[:, cols] = jnp.where(lane < 64, d_v_parts[0], d_v_parts[1]).astype(low)
        d_k.append(jnp.where(lane < 64, d_k_parts[0], d_k_parts[1]) * 0.125)
        d_q.append(jnp.concatenate(d_q_parts, 0).T * 0.125)
    d_q = jnp.concatenate(d_q, 1)
    d_k = jnp.concatenate(d_k, 1)
    cosine, sine = angle_tables(tab_ref)
    low_half = lane_masks(slots)
    signed = jnp.where(low_half, sine, -sine)
    dq_low = (d_q * cosine + partner(d_q, low_half) * signed).astype(low)
    dk_low = (d_k * cosine + partner(d_k, low_half) * signed).astype(low)
    dq_ref[...] = dq_low
    dk_ref[...] = dk_low
    turned = d_q * partner(q_ref[...].astype(single), low_half)
    turned = turned + d_k * partner(k_ref[...].astype(single), low_half)
    turned = jnp.where(low_half, -turned, turned)
    sum_ref[0:1, :] = jnp.sum(turned * row_ref[:, 0:1], 0, keepdims=True)
    sum_ref[1:2, :] = jnp.sum(turned * row_ref[:, 1:2], 0, keepdims=True)
    sum_ref[2:3, :] = jnp.sum(dq_low.astype(single), 0, keepdims=True)
    sum_ref[3:4, :] = jnp.sum(dk_low.astype(single), 0, keepdims=True)
    sum_ref[4:5, :] = jnp.sum(dv_ref[...].astype(single), 0, keepdims=True)
    sum_ref[5:8, :] = jnp.zeros((3, GROUP), single)


def attend_back(d_attn, weight, q, k, v, probs, tables, places):
    slots, width = d_attn.shape
    steps = width // GROUP
    low = jnp.bfloat16
    heads = GROUP // 64
    cols = pl.BlockSpec((slots, GROUP), lambda j: (0, j))
    act = jax.ShapeDtypeStruct((slots, width), low)
    return pl.pallas_call(
        attend_back_kernel,
        grid=(steps,),
        in_specs=[
            pl.BlockSpec((slots, width), lambda j: (0, 0)),
            pl.BlockSpec((GROUP, width), lambda j: (j, 0)),
            cols,
            cols,
            cols,
            pl.BlockSpec((heads, slots, slots), lambda j: (j, 0, 0)),
            pl.BlockSpec((4, GRID, GROUP), lambda j: (0, 0, j)),
            pl.BlockSpec((slots, 2), lambda j: (0, 0)),
        ],
        out_specs=[cols] * 3 + [pl.BlockSpec((8, GROUP), lambda j: (0, j))],
        out_shape=[act] * 3 + [jax.ShapeDtypeStruct((8, width), jnp.float32)],
        cost_estimate=pl.CostEstimate(
            flops=2 * slots * width * width + 12 * slots * slots * width,
            bytes_accessed=width * width * 2 + slots * slots * 24,
            transcendentals=0,
        ),
        name="attend_back",
    )(d_attn, weight, q, k, v, probs, tables, places)


def swap(values, axis, bit):
    total = lax.axis_size(axis)
    return lax.ppermute(values, axis, [(i, i ^ bit) for i in range(total)])


def halve(values, axis, bit, at):
    mine = (lax.axis_index(axis) // bit) % 2
    away = lax.dynamic_index_in_dim(values, 1 - mine, at, keepdims=False)
    kept = lax.dynamic_index_in_dim(values, mine, at, keepdims=False)
    single = jnp.float32
    got = swap(away, axis, bit)
    return (kept.astype(single) + got.astype(single)).astype(values.dtype)


def join(values, axis, bit, at):
    mine = (lax.axis_index(axis) // bit) % 2
    got = swap(values, axis, bit)
    first = jnp.where(mine == 0, values, got)
    second = jnp.where(mine == 0, got, values)
    return jnp.concatenate([first, second], at)


def matrix_sum(left, right):
    single, low = jnp.float32, jnp.bfloat16
    shares = lax.axis_size("img")
    core = lax.axis_index("band") % 2
    half = right.shape[1] // 2

    def product(which):
        part = lax.dynamic_slice_in_dim(right, which * half, half, 1)
        return jnp.einsum("qa,qb->ab", left, part, preferred_element_type=single).astype(low)

    got = swap(product(1 - core), "band", 1)
    total = (product(core).astype(single) + got.astype(single)).astype(low)
    depth = left.shape[1] // shares
    total = halve(total.reshape(shares, 2, depth // 2, half), "band", 2, 1)
    bit = 1
    while bit < shares:
        total = total.reshape(shares // (2 * bit), 2, depth // 2, half)
        total = halve(total, "img", bit, 1)
        bit *= 2
    total = total.reshape(depth // 2, half)
    total = join(total, "band", 2, 0)
    total = join(total, "band", 1, 1)
    return total.astype(single)


def vector_sum(values):
    for axis in ("band", "img"):
        bit = 1
        while bit < lax.axis_size(axis):
            values = values + swap(values, axis, bit)
            bit *= 2
    return values


def local(
    patches,
    patch_mask,
    band_first,
    attn_gain,
    attn_shift,
    inproj_weight,
    inproj_bias,
    rotary_freqs,
    outproj_weight,
    outproj_bias,
    mlp_gain,
    mlp_shift,
    expand_weight,
    expand_bias,
    reduce_weight,
    reduce_bias,
    cotangent,
):
    single = jnp.float32
    low = jnp.bfloat16
    images, slots, width = patches.shape
    heads = rotary_freqs.shape[1]
    size = width // heads
    bands = lax.axis_size("band")
    here = lax.axis_index("band")

    count = images // bands
    total = slots * bands

    def gather_image(values):
        pieces = lax.all_to_all(
            values.reshape(bands, count, slots, width), "band", 0, 0, tiled=True
        )
        return jnp.swapaxes(pieces, 0, 1).reshape(count, total, width)

    def spread_image(values):
        pieces = jnp.swapaxes(values.reshape(count, bands, slots, width), 0, 1)
        pieces = lax.all_to_all(pieces, "band", 0, 0, tiled=True)
        return pieces.reshape(images, slots, width)

    def flatten(values):
        return values.reshape(-1, values.shape[-1])

    patches = gather_image(patches)
    cotangent = gather_image(cotangent)
    starts = lax.dynamic_slice_in_dim(band_first, here * count, count, 0)
    row_in = jnp.arange(slots) // GRID
    side = 4 * starts[:, -1:] // 3
    counts = jnp.concatenate([starts[:, 1:], side], 1) - starts
    live = (row_in[None, None, :] < counts[:, :, None]) & (
        jnp.arange(slots)[None, None, :] % GRID < side[:, :, None]
    )
    mask = live.reshape(count, total).astype(single)
    rows = (starts[:, :, None] + row_in[None, None, :]).reshape(count, total).astype(single)
    cols = jnp.broadcast_to(
        (jnp.arange(total) % GRID).astype(single)[None, :], rows.shape
    )
    freqs = rotary_freqs.astype(single)
    lanes = jnp.concatenate([freqs, freqs], -1).reshape(2, width)
    row_angle = rows[:, ::GRID, None] * lanes[0]
    col_angle = jnp.broadcast_to(
        jnp.arange(GRID, dtype=single)[None, :, None] * lanes[1], row_angle.shape
    )
    tables = jnp.stack(
        [jnp.cos(row_angle), jnp.sin(row_angle), jnp.cos(col_angle), jnp.sin(col_angle)], 1
    )
    hide = jnp.where(mask > 0, 0.0, NEG).astype(single)[..., None]
    places = jnp.stack([rows, cols], -1)

    wide = patches.astype(single)
    xhat_one, rstd_one = norm_parts(wide)
    gain_one = attn_gain.astype(single)
    attn_in = (xhat_one * gain_one + attn_shift.astype(single)).astype(low)
    pieces = [
        attend(attn_in[i], inproj_weight, inproj_bias, tables[i], hide[i]) for i in range(count)
    ]
    query_rot, key_rot, value_low, mix, probs = (jnp.stack(p) for p in zip(*pieces))
    attn_out = jnp.dot(mix, outproj_weight, preferred_element_type=single)
    resid_mid = wide + attn_out + outproj_bias.astype(single)
    xhat_two, rstd_two = norm_parts(resid_mid)
    gain_two = mlp_gain.astype(single)
    mlp_in = (xhat_two * gain_two + mlp_shift.astype(single)).astype(low)
    pre_act = jnp.dot(mlp_in, expand_weight, preferred_element_type=single)
    pre_act = pre_act + expand_bias.astype(single)
    half_erf = 0.5 + 0.5 * lax.erf(pre_act * (0.5**0.5))
    hidden = (pre_act * half_erf).astype(low)
    slope = half_erf + pre_act * jnp.exp(-0.5 * pre_act * pre_act) * 0.3989422804014327
    branch = jnp.dot(hidden, reduce_weight, preferred_element_type=single)
    block_out = mask[..., None] * (resid_mid + branch + reduce_bias.astype(single))
    block_out = spread_image(block_out.astype(low))

    grad_top = cotangent.astype(single) * mask[..., None]
    grad_low = grad_top.astype(low)
    grad_reduce_weight = matrix_sum(flatten(hidden), flatten(grad_low))
    grad_reduce_bias = jnp.sum(grad_top, (0, 1))
    d_hidden = jnp.einsum("iqd,fd->iqf", grad_low, reduce_weight, preferred_element_type=single)
    d_pre = (d_hidden * slope).astype(low)
    grad_expand_weight = matrix_sum(flatten(mlp_in), flatten(d_pre))
    grad_expand_bias = jnp.sum(d_pre.astype(single), (0, 1))
    d_mlp_in = jnp.einsum("iqf,df->iqd", d_pre, expand_weight, preferred_element_type=single)
    grad_mlp_gain = jnp.sum(d_mlp_in * xhat_two, (0, 1))
    grad_mlp_shift = jnp.sum(d_mlp_in, (0, 1))
    d_mid = grad_top + norm_back(d_mlp_in, gain_two, xhat_two, rstd_two)
    d_attn = d_mid.astype(low)
    grad_outproj_weight = matrix_sum(flatten(mix), flatten(d_attn))
    grad_outproj_bias = jnp.sum(d_attn.astype(single), (0, 1))
    pieces = [
        attend_back(
            d_attn[i],
            outproj_weight,
            query_rot[i],
            key_rot[i],
            value_low[i],
            probs[i],
            tables[i],
            places[i],
        )
        for i in range(count)
    ]
    d_queries, d_keys, d_values, parts = (jnp.stack(p) for p in zip(*pieces))
    parts = jnp.sum(parts, 0)
    grad_freqs = jnp.sum(parts[:2].reshape(2, heads, 2, size // 2), 2)
    grad_inproj_bias = parts[2:5].reshape(-1)
    d_proj = jnp.concatenate([d_queries, d_keys, d_values], -1)
    grad_inproj_weight = matrix_sum(flatten(attn_in), flatten(d_proj))
    d_attn_in = jnp.einsum("iqe,de->iqd", d_proj, inproj_weight, preferred_element_type=single)
    grad_attn_gain = jnp.sum(d_attn_in * xhat_one, (0, 1))
    grad_attn_shift = jnp.sum(d_attn_in, (0, 1))
    d_patches = d_mid + norm_back(d_attn_in, gain_one, xhat_one, rstd_one)
    d_patches = spread_image(d_patches.astype(low))

    small = (
        grad_attn_gain,
        grad_attn_shift,
        grad_inproj_bias,
        grad_outproj_bias,
        grad_mlp_gain,
        grad_mlp_shift,
        grad_expand_bias,
        grad_reduce_bias,
        grad_freqs.reshape(-1),
    )
    packed = vector_sum(jnp.concatenate(small))
    shares = lax.axis_size("img")
    mine = lax.axis_index("img")
    sums = []
    at = 0
    for piece in small:
        long = piece.shape[0]
        sums.append(packed[at : at + long])
        at += long
    freq_total = sums.pop().reshape(grad_freqs.shape)
    sums = [
        lax.dynamic_slice_in_dim(s, mine * (s.shape[0] // shares), s.shape[0] // shares)
        for s in sums
    ]
    return (
        block_out,
        d_patches,
        sums[0],
        sums[1],
        grad_inproj_weight,
        sums[2],
        freq_total,
        grad_outproj_weight,
        sums[3],
        sums[4],
        sums[5],
        grad_expand_weight,
        sums[6],
        grad_reduce_weight,
        sums[7],
    )


def solution(mesh):
    act = P("img", "band", None)
    row = P("img")
    mat = P("img", None)
    return jax.shard_map(
        local,
        mesh=mesh,
        in_specs=(act, P("img", "band"), P("img", None)) + (P(),) * 13 + (act,),
        out_specs=(act, act, row, row, mat, row, P(), mat, row, row, row, mat, row, mat, row),
        check_vma=False,
    )
```

```python
import jax
import jax.numpy as jnp
from jax import lax
from jax.experimental import pallas as pl
from jax.experimental.pallas import tpu as pltpu
from jax.sharding import PartitionSpec as P

GRID = 24
EPS = 1e-06
NEG = -1e30


def norm_parts(values):
    center = values - jnp.mean(values, -1, keepdims=True)
    rstd = lax.rsqrt(jnp.mean(center * center, -1, keepdims=True) + EPS)
    return center * rstd, rstd


def norm_back(grad, gain, xhat, rstd):
    scaled = grad * gain
    inner = jnp.mean(scaled * xhat, -1, keepdims=True)
    return rstd * (scaled - jnp.mean(scaled, -1, keepdims=True) - xhat * inner)


GROUP = 256


def contract(left, right, left_dim, right_dim):
    return lax.dot_general(
        left, right, (((left_dim,), (right_dim,)), ((), ())), preferred_element_type=jnp.float32
    )


def partner(values, low_half):
    wide = values.shape[-1]
    return jnp.where(
        low_half, pltpu.roll(values, wide - 32, 1), pltpu.roll(values, 32, 1)
    )


def angle_tables(tables):
    row_cos, row_sin, col_cos, col_sin = (tables[i] for i in range(4))
    count, wide = row_cos.shape
    rc, rs = row_cos[:, None, :], row_sin[:, None, :]
    cc, cs = col_cos[None, :, :], col_sin[None, :, :]
    cosine = (rc * cc - rs * cs).reshape(count * count, wide)
    sine = (rs * cc + rc * cs).reshape(count * count, wide)
    return cosine, sine


def lane_masks(slots):
    lane = lax.broadcasted_iota(jnp.int32, (slots, GROUP), 1)
    return lane % 64 < 32


def attend_kernel(
    x_ref, wq_ref, wk_ref, wv_ref, b_ref, tab_ref, bias_ref, q_ref, k_ref, v_ref, mix_ref, p_ref
):
    low, single = jnp.bfloat16, jnp.float32
    slots = x_ref.shape[0]
    cosine, sine = angle_tables(tab_ref)
    low_half = lane_masks(slots)
    signed = jnp.where(low_half, -sine, sine)
    x = x_ref[...]

    def projected(w_ref, at):
        return jnp.dot(x, w_ref[...], preferred_element_type=single) + b_ref[at].astype(single)

    q = projected(wq_ref, 0)
    q_ref[...] = ((q * cosine + partner(q, low_half) * signed)).astype(low)
    k = projected(wk_ref, 1)
    k_ref[...] = (k * cosine + partner(k, low_half) * signed).astype(low)
    v_ref[...] = projected(wv_ref, 2).astype(low)
    hide = bias_ref[...]
    lane = lax.broadcasted_iota(jnp.int32, (slots, 128), 1)
    for pair in range(GROUP // 128):
        cols = slice(pair * 128, pair * 128 + 128)
        q = q_ref[:, cols] * jnp.asarray(0.125, low)
        k = k_ref[:, cols]
        v_turned = v_ref[:, cols].T
        parts = []
        for head in range(2):
            own = (lane < 64) if head == 0 else (lane >= 64)
            scores = contract(k, jnp.where(own, q, jnp.zeros_like(q)), 1, 1) + hide
            expo = jnp.exp(scores - jnp.max(scores, 0, keepdims=True))
            probs = (expo * (1.0 / jnp.sum(expo, 0, keepdims=True))).astype(low)
            p_ref[pair * 2 + head] = probs
            rows = slice(head * 64, head * 64 + 64)
            parts.append(jnp.dot(v_turned[rows], probs, preferred_element_type=single))
        mix_ref[:, cols] = jnp.concatenate(parts, 0).T.astype(low)


def attend(attn_in, weight, bias, tables, hide):
    slots, width = attn_in.shape
    steps = width // GROUP
    low = jnp.bfloat16

    def part(at):
        return pl.BlockSpec((width, GROUP), lambda j: (0, at * steps + j))

    cols = pl.BlockSpec((slots, GROUP), lambda j: (0, j))
    act = jax.ShapeDtypeStruct((slots, width), low)
    heads = GROUP // 64
    return pl.pallas_call(
        attend_kernel,
        grid=(steps,),
        in_specs=[
            pl.BlockSpec((slots, width), lambda j: (0, 0)),
            part(0),
            part(1),
            part(2),
            pl.BlockSpec((3, 1, GROUP), lambda j: (0, 0, j)),
            pl.BlockSpec((4, GRID, GROUP), lambda j: (0, 0, j)),
            pl.BlockSpec((slots, 1), lambda j: (0, 0)),
        ],
        out_specs=[cols] * 4 + [pl.BlockSpec((heads, slots, slots), lambda j: (j, 0, 0))],
        out_shape=[act] * 4 + [jax.ShapeDtypeStruct((width // 64, slots, slots), low)],
        cost_estimate=pl.CostEstimate(
            flops=6 * slots * width * width + 4 * slots * slots * width,
            bytes_accessed=3 * width * width * 2 + slots * slots * 24,
            transcendentals=slots * slots * 12,
        ),
        name="attend",
    )(attn_in, weight, weight, weight, bias.reshape(3, 1, width), tables, hide)


def attend_back_kernel(
    g_ref, wo_ref, q_ref, k_ref, v_ref, p_ref, tab_ref, row_ref, dq_ref, dk_ref, dv_ref, sum_ref
):
    low, single = jnp.bfloat16, jnp.float32
    slots = g_ref.shape[0]
    d_mix = contract(g_ref[...], wo_ref[...], 1, 1).astype(low)
    lane = lax.broadcasted_iota(jnp.int32, (slots, 128), 1)
    zero = jnp.zeros((slots, 128), low)
    d_q, d_k = [], []
    for pair in range(GROUP // 128):
        cols = slice(pair * 128, pair * 128 + 128)
        q, k, v = q_ref[:, cols], k_ref[:, cols], v_ref[:, cols]
        grad = d_mix[:, cols]
        k_turned = k.T
        d_v_parts, d_k_parts, d_q_parts = [], [], []
        for head in range(2):
            own = (lane < 64) if head == 0 else (lane >= 64)
            probs = p_ref[pair * 2 + head]
            wide = probs.astype(single)
            d_probs = contract(v, jnp.where(own, grad, zero), 1, 1)
            weighed = wide * d_probs
            inner = jnp.sum(weighed, 0, keepdims=True)
            d_scores = (weighed - wide * inner).astype(low)
            d_v_parts.append(jnp.dot(probs, grad, preferred_element_type=single))
            d_k_parts.append(jnp.dot(d_scores, q, preferred_element_type=single))
            rows = slice(head * 64, head * 64 + 64)
            d_q_parts.append(jnp.dot(k_turned[rows], d_scores, preferred_element_type=single))
        dv_ref[:, cols] = jnp.where(lane < 64, d_v_parts[0], d_v_parts[1]).astype(low)
        d_k.append(jnp.where(lane < 64, d_k_parts[0], d_k_parts[1]) * 0.125)
        d_q.append(jnp.concatenate(d_q_parts, 0).T * 0.125)
    d_q = jnp.concatenate(d_q, 1)
    d_k = jnp.concatenate(d_k, 1)
    cosine, sine = angle_tables(tab_ref)
    low_half = lane_masks(slots)
    signed = jnp.where(low_half, sine, -sine)
    dq_low = (d_q * cosine + partner(d_q, low_half) * signed).astype(low)
    dk_low = (d_k * cosine + partner(d_k, low_half) * signed).astype(low)
    dq_ref[...] = dq_low
    dk_ref[...] = dk_low
    turned = d_q * partner(q_ref[...].astype(single), low_half)
    turned = turned + d_k * partner(k_ref[...].astype(single), low_half)
    turned = jnp.where(low_half, -turned, turned)
    sum_ref[0:1, :] = jnp.sum(turned * row_ref[:, 0:1], 0, keepdims=True)
    sum_ref[1:2, :] = jnp.sum(turned * row_ref[:, 1:2], 0, keepdims=True)
    sum_ref[2:3, :] = jnp.sum(dq_low.astype(single), 0, keepdims=True)
    sum_ref[3:4, :] = jnp.sum(dk_low.astype(single), 0, keepdims=True)
    sum_ref[4:5, :] = jnp.sum(dv_ref[...].astype(single), 0, keepdims=True)
    sum_ref[5:8, :] = jnp.zeros((3, GROUP), single)


def attend_back(d_attn, weight, q, k, v, probs, tables, places):
    slots, width = d_attn.shape
    steps = width // GROUP
    low = jnp.bfloat16
    heads = GROUP // 64
    cols = pl.BlockSpec((slots, GROUP), lambda j: (0, j))
    act = jax.ShapeDtypeStruct((slots, width), low)
    return pl.pallas_call(
        attend_back_kernel,
        grid=(steps,),
        in_specs=[
            pl.BlockSpec((slots, width), lambda j: (0, 0)),
            pl.BlockSpec((GROUP, width), lambda j: (j, 0)),
            cols,
            cols,
            cols,
            pl.BlockSpec((heads, slots, slots), lambda j: (j, 0, 0)),
            pl.BlockSpec((4, GRID, GROUP), lambda j: (0, 0, j)),
            pl.BlockSpec((slots, 2), lambda j: (0, 0)),
        ],
        out_specs=[cols] * 3 + [pl.BlockSpec((8, GROUP), lambda j: (0, j))],
        out_shape=[act] * 3 + [jax.ShapeDtypeStruct((8, width), jnp.float32)],
        cost_estimate=pl.CostEstimate(
            flops=2 * slots * width * width + 12 * slots * slots * width,
            bytes_accessed=width * width * 2 + slots * slots * 24,
            transcendentals=0,
        ),
        name="attend_back",
    )(d_attn, weight, q, k, v, probs, tables, places)


def swap(values, axis, bit):
    total = lax.axis_size(axis)
    return lax.ppermute(values, axis, [(i, i ^ bit) for i in range(total)])


def pick(values, axis, bit, at, other):
    mine = (lax.axis_index(axis) // bit) % 2
    return lax.dynamic_index_in_dim(values, 1 - mine if other else mine, at, keepdims=False)


def join(values, axis, bit, at):
    mine = (lax.axis_index(axis) // bit) % 2
    got = swap(values, axis, bit)
    first = jnp.where(mine == 0, values, got)
    second = jnp.where(mine == 0, got, values)
    return jnp.concatenate([first, second], at)


def add_low(first, second):
    total = first.astype(jnp.float32) + second.astype(jnp.float32)
    return total.astype(jnp.bfloat16)


CORE, CHIP = ("band", 1), ("band", 2)


class Chain:
    def __init__(self, left, right, start, count):
        core = lax.axis_index("band") % 2
        half = right.shape[1] // 2
        shares = lax.axis_size("img")
        depth = left.shape[1] // shares
        bits = []
        bit = 1
        while bit < shares:
            bits.insert(0, ("img", bit))
            bit *= 2
        self.keys = bits + [CHIP]
        shape = (2,) * len(self.keys) + (depth // 2, count)

        def product(which):
            part = lax.dynamic_slice_in_dim(right, which * half + start, count, 1)
            full = jnp.einsum("qa,qb->ab", left, part, preferred_element_type=jnp.float32)
            return full.astype(jnp.bfloat16)

        self.got = swap(product(1 - core), *CORE).reshape(shape)
        self.kept = product(core).reshape(shape)

    def step(self, key):
        at = self.keys.index(key)
        away = add_low(pick(self.kept, *key, at, True), pick(self.got, *key, at, True))
        got = swap(away, *key)
        self.kept = add_low(pick(self.kept, *key, at, False), pick(self.got, *key, at, False))
        self.got = got
        self.keys.remove(key)

    def finish(self):
        for key in self.keys[::-1]:
            self.step(key)
        total = join(add_low(self.kept, self.got), *CHIP, 0)
        return join(total[:, None, :], *CORE, 1)


def tie(value, *chains):
    held = lax.optimization_barrier((value, *(c.kept for c in chains)))
    for chain, kept in zip(chains, held[1:]):
        chain.kept = kept
    return held[0]


def merged(*chains):
    total = jnp.concatenate([c.finish() for c in chains], -1)
    return total.reshape(total.shape[0], -1).astype(jnp.float32)


def vector_sum(values):
    for axis in ("band", "img"):
        bit = 1
        while bit < lax.axis_size(axis):
            values = values + swap(values, axis, bit)
            bit *= 2
    return values


def local(
    patches,
    patch_mask,
    band_first,
    attn_gain,
    attn_shift,
    inproj_weight,
    inproj_bias,
    rotary_freqs,
    outproj_weight,
    outproj_bias,
    mlp_gain,
    mlp_shift,
    expand_weight,
    expand_bias,
    reduce_weight,
    reduce_bias,
    cotangent,
):
    single = jnp.float32
    low = jnp.bfloat16
    images, slots, width = patches.shape
    heads = rotary_freqs.shape[1]
    size = width // heads
    bands = lax.axis_size("band")
    here = lax.axis_index("band")

    count = images // bands
    total = slots * bands

    def gather_image(values):
        pieces = lax.all_to_all(
            values.reshape(bands, count, slots, width), "band", 0, 0, tiled=True
        )
        return jnp.swapaxes(pieces, 0, 1).reshape(count, total, width)

    def spread_image(values):
        pieces = jnp.swapaxes(values.reshape(count, bands, slots, width), 0, 1)
        pieces = lax.all_to_all(pieces, "band", 0, 0, tiled=True)
        return pieces.reshape(images, slots, width)

    def flatten(values):
        return values.reshape(-1, values.shape[-1])

    patches = gather_image(patches)
    cotangent = gather_image(cotangent)
    starts = lax.dynamic_slice_in_dim(band_first, here * count, count, 0)
    row_in = jnp.arange(slots) // GRID
    side = 4 * starts[:, -1:] // 3
    counts = jnp.concatenate([starts[:, 1:], side], 1) - starts
    live = (row_in[None, None, :] < counts[:, :, None]) & (
        jnp.arange(slots)[None, None, :] % GRID < side[:, :, None]
    )
    mask = live.reshape(count, total).astype(single)
    rows = (starts[:, :, None] + row_in[None, None, :]).reshape(count, total).astype(single)
    cols = jnp.broadcast_to(
        (jnp.arange(total) % GRID).astype(single)[None, :], rows.shape
    )
    freqs = rotary_freqs.astype(single)
    lanes = jnp.concatenate([freqs, freqs], -1).reshape(2, width)
    row_angle = rows[:, ::GRID, None] * lanes[0]
    col_angle = jnp.broadcast_to(
        jnp.arange(GRID, dtype=single)[None, :, None] * lanes[1], row_angle.shape
    )
    tables = jnp.stack(
        [jnp.cos(row_angle), jnp.sin(row_angle), jnp.cos(col_angle), jnp.sin(col_angle)], 1
    )
    hide = jnp.where(mask > 0, 0.0, NEG).astype(single)[..., None]
    places = jnp.stack([rows, cols], -1)

    wide = patches.astype(single)
    xhat_one, rstd_one = norm_parts(wide)
    gain_one = attn_gain.astype(single)
    attn_in = (xhat_one * gain_one + attn_shift.astype(single)).astype(low)
    pieces = [
        attend(attn_in[i], inproj_weight, inproj_bias, tables[i], hide[i]) for i in range(count)
    ]
    query_rot, key_rot, value_low, mix, probs = (jnp.stack(p) for p in zip(*pieces))
    attn_out = jnp.dot(mix, outproj_weight, preferred_element_type=single)
    resid_mid = wide + attn_out + outproj_bias.astype(single)
    xhat_two, rstd_two = norm_parts(resid_mid)
    gain_two = mlp_gain.astype(single)
    mlp_in = (xhat_two * gain_two + mlp_shift.astype(single)).astype(low)
    pre_act = jnp.dot(mlp_in, expand_weight, preferred_element_type=single)
    pre_act = pre_act + expand_bias.astype(single)
    half_erf = 0.5 + 0.5 * lax.erf(pre_act * (0.5**0.5))
    hidden = (pre_act * half_erf).astype(low)
    slope = half_erf + pre_act * jnp.exp(-0.5 * pre_act * pre_act) * 0.3989422804014327
    branch = jnp.dot(hidden, reduce_weight, preferred_element_type=single)
    block_out = mask[..., None] * (resid_mid + branch + reduce_bias.astype(single))
    block_out = spread_image(block_out.astype(low))

    grad_top = cotangent.astype(single) * mask[..., None]
    grad_low = grad_top.astype(low)
    side_bit = ("img", 1)
    sum_reduce = Chain(flatten(hidden), flatten(grad_low), 0, width // 2)
    grad_low = tie(grad_low, sum_reduce)
    grad_reduce_bias = jnp.sum(grad_top, (0, 1))
    d_hidden = jnp.einsum("iqd,fd->iqf", grad_low, reduce_weight, preferred_element_type=single)
    d_pre = (d_hidden * slope).astype(low)
    sum_expand = Chain(flatten(mlp_in), flatten(d_pre), 0, d_pre.shape[-1] // 2)
    d_pre = tie(d_pre, sum_expand)
    grad_expand_bias = jnp.sum(d_pre.astype(single), (0, 1))
    d_mlp_in = jnp.einsum("iqf,df->iqd", d_pre, expand_weight, preferred_element_type=single)
    grad_mlp_gain = jnp.sum(d_mlp_in * xhat_two, (0, 1))
    grad_mlp_shift = jnp.sum(d_mlp_in, (0, 1))
    d_mid = grad_top + norm_back(d_mlp_in, gain_two, xhat_two, rstd_two)
    d_attn = d_mid.astype(low)
    sum_outproj = Chain(flatten(mix), flatten(d_attn), 0, width // 2)
    sum_reduce.step(CHIP)
    sum_expand.step(side_bit)
    d_attn = tie(d_attn, sum_outproj, sum_reduce, sum_expand)
    grad_outproj_bias = jnp.sum(d_attn.astype(single), (0, 1))
    pieces = [
        attend_back(
            d_attn[i],
            outproj_weight,
            query_rot[i],
            key_rot[i],
            value_low[i],
            probs[i],
            tables[i],
            places[i],
        )
        for i in range(count)
    ]
    d_queries, d_keys, d_values, parts = (jnp.stack(p) for p in zip(*pieces))
    parts = jnp.sum(parts, 0)
    grad_freqs = jnp.sum(parts[:2].reshape(2, heads, 2, size // 2), 2)
    grad_inproj_bias = parts[2:5].reshape(-1)
    d_proj = jnp.concatenate([d_queries, d_keys, d_values], -1)
    lead = (width * 3 // 2) * 5 // 9
    sum_first = Chain(flatten(attn_in), flatten(d_proj), 0, lead)
    sum_second = Chain(flatten(attn_in), flatten(d_proj), lead, width * 3 // 2 - lead)
    sum_first.step(CHIP)
    sum_second.step(side_bit)
    d_attn_in = jnp.einsum("iqe,de->iqd", d_proj, inproj_weight, preferred_element_type=single)
    grad_attn_gain = jnp.sum(d_attn_in * xhat_one, (0, 1))
    grad_attn_shift = jnp.sum(d_attn_in, (0, 1))
    d_patches = d_mid + norm_back(d_attn_in, gain_one, xhat_one, rstd_one)
    d_patches = spread_image(d_patches.astype(low))

    small = (
        grad_attn_gain,
        grad_attn_shift,
        grad_inproj_bias,
        grad_outproj_bias,
        grad_mlp_gain,
        grad_mlp_shift,
        grad_expand_bias,
        grad_reduce_bias,
        grad_freqs.reshape(-1),
    )
    shares = lax.axis_size("img")
    packed = jnp.concatenate([piece.reshape(shares, -1) for piece in small], 1)
    packed = vector_sum(packed)
    freq_at = packed.shape[1] - grad_freqs.size // shares
    freq_total = packed[:, freq_at:].reshape(grad_freqs.shape)
    own = lax.dynamic_index_in_dim(packed, lax.axis_index("img"), 0, keepdims=False)
    sums = []
    at = 0
    for piece in small[:-1]:
        long = piece.shape[0] // shares
        sums.append(own[at : at + long])
        at += long
    return (
        block_out,
        d_patches,
        sums[0],
        sums[1],
        merged(sum_first, sum_second),
        sums[2],
        freq_total,
        merged(sum_outproj),
        sums[3],
        sums[4],
        sums[5],
        merged(sum_expand),
        sums[6],
        merged(sum_reduce),
        sums[7],
    )


def solution(mesh):
    act = P("img", "band", None)
    row = P("img")
    mat = P("img", None)
    return jax.shard_map(
        local,
        mesh=mesh,
        in_specs=(act, P("img", "band"), P("img", None)) + (P(),) * 13 + (act,),
        out_specs=(act, act, row, row, mat, row, P(), mat, row, row, row, mat, row, mat, row),
        check_vma=False,
    )
```
